32 devices in a mesh: band: 4 (over x, core), slab: 8 (over z, y).
Axes of the slice: x: 2, y: 2, z: 4, core: 2. Of those that a mesh axis runs over, the one named last changes fastest.
Arguments:
- orbitals: float32 [12, 128, 128, 128], P('band', 'slab'), may hold values from -6 to 6
- occupation: float32 [12], replicated, may hold values from 0.2 to 2
- assignment: int32 [12], P('band'), may hold values from 0 to 11, each once
- pair_live: int32 [12, 12], P('band'), may hold values from 0 to 1, as said below
Outputs:
- exchange: float32 [12, 128, 128, 128], P('band', 'slab')
The draws below stay inside these ranges and needn't reach their ends.
Inputs may be any that keep to these rules, and one draw needn't show every extreme that they name: `assignment`: every band number appears in exactly one slot. pair_live[s, t] equals pair_live[t, s].
All inputs are finite; a program needn't handle non-finite values.
Results may differ from the reference program's by a relative error of at most 0.00016.
Values sent between devices are 32-bit elements; how exact they have to be, the bound alone decides.
A program may use at most 64 MiB of HBM per device.

```python
import jax
import jax.numpy as jnp
from jax import lax

GRID = 128
ORB_GRP = 3
ORBITALS = 12
N_BAND = 4


def draw_pair_live(key, part):
    picks = jax.random.randint(key, (ORBITALS, ORBITALS), 0, 4)
    strict = jnp.triu(picks, 1)
    mirrored = strict + strict.T
    return jnp.minimum(mirrored, 1).astype(jnp.int32)


def steps_of(rng, dims, shards, smallest, high):
    level, own = 1.0, jax.random.fold_in(rng, 6)
    for dim, shards_of in shards:
        steps = jnp.exp(jax.random.uniform(jax.random.fold_in(own, dim), (shards_of,), jnp.float32, smallest / len(shards), high / len(shards)))
        level = level * jnp.repeat(steps, dims[dim] // shards_of).reshape([-1 if axis == dim else 1 for axis in range(len(dims))])
    return level


def centred(rng, shape, width, reach, split=(), kind=jnp.bfloat16):
    level = steps_of(rng, shape, split, -0.22, 0.18) if split else 1.0
    entries = jax.random.normal(rng, shape, jnp.float32) * width * level
    return jnp.minimum(jnp.maximum(entries, -reach), reach).astype(kind)


def setup_inputs(seed: int = 0) -> dict:
    seeds = jax.random.split(jax.random.key(seed), 5)
    orbitals = centred(seeds[0], (ORBITALS, GRID, GRID, GRID), 1.0, 6.0, ((0, 4), (1, 8)), jnp.float32)
    occupation = jnp.clip(jax.random.uniform(seeds[1], (ORBITALS,), jnp.float32, 0.2, 2.0), 0.2, 2.0)
    assignment = jax.random.permutation(seeds[2], ORBITALS).astype(jnp.int32)
    pair_live = draw_pair_live(jax.random.fold_in(seeds[4], 71), 0)
    return {"orbitals": orbitals, "occupation": occupation, "assignment": assignment, "pair_live": pair_live}


highest = lax.Precision.HIGHEST
screening = 0.01
lateral = 0.01

def sine_table(points):
    numbers = jnp.arange(points, dtype=jnp.float32) + 1.0
    return jnp.sqrt(2.0 / (points + 1.0)) * jnp.sin(jnp.pi * numbers[:, None] * numbers[None, :] / (points + 1.0))

def eigen_values(points):
    numbers = jnp.arange(points, dtype=jnp.float32) + 1.0
    return 2.0 - 2.0 * jnp.cos(jnp.pi * numbers / (points + 1.0))

def screened_solve(density):
    points = density.shape[-1]
    sine_rows = sine_table(points)
    spectra = jnp.einsum('pzyx,ax->pzya', density, sine_rows, precision=highest)
    spectra = jnp.einsum('pzya,by->pzba', spectra, sine_rows, precision=highest)
    spectra = jnp.einsum('pzba,cz->pcba', spectra, sine_rows, precision=highest)
    eigen_list = eigen_values(points)
    spectra = spectra / (eigen_list[:, None, None] + lateral * (eigen_list[None, :, None] + eigen_list[None, None, :]) + screening)
    spectra = jnp.einsum('pcba,cz->pzba', spectra, sine_rows, precision=highest)
    spectra = jnp.einsum('pzba,by->pzya', spectra, sine_rows, precision=highest)
    return jnp.einsum('pzya,ax->pzyx', spectra, sine_rows, precision=highest)

def reference(orbitals, occupation, assignment, pair_live):
    weights = occupation[assignment]
    live_pairs = pair_live.astype(jnp.float32)
    exchange_sum = jnp.zeros_like(orbitals)
    members = jnp.arange(ORB_GRP, dtype=jnp.int32)
    for block_index in range(N_BAND):
        neighbour = (block_index + 1) % N_BAND
        start_slot = neighbour * ORB_GRP
        visitors = orbitals[start_slot:start_slot + ORB_GRP]
        visit_weight = weights[start_slot:start_slot + ORB_GRP]

        def per_member(running, member):
            slot_index = block_index * ORB_GRP + member
            resident = lax.dynamic_index_in_dim(orbitals, slot_index, 0, keepdims=False)
            potential = screened_solve(resident[None] * visitors)
            live_row = lax.dynamic_index_in_dim(live_pairs, slot_index, 0, keepdims=False)[start_slot:start_slot + ORB_GRP]
            own_term = -lax.optimization_barrier(jnp.sum((live_row * visit_weight)[:, None, None, None] * potential * visitors, axis=0))
            resident_weight = lax.dynamic_index_in_dim(weights, slot_index, 0, keepdims=False)
            visit_term = -(live_row * resident_weight)[:, None, None, None] * potential * resident[None]
            running = running.at[slot_index].add(own_term)
            running = running.at[start_slot:start_slot + ORB_GRP].add(visit_term)
            return (running, None)
        exchange_sum, _ = lax.scan(per_member, exchange_sum, members)
    return exchange_sum
```

```python
import functools

import jax
import jax.numpy as jnp
import numpy as np
from jax import lax
from jax.experimental import pallas as pl
from jax.experimental.pallas import tpu as pltpu
from jax.sharding import PartitionSpec as P

screening = 0.01
lateral = 0.01
MESH = pl.DeviceIdType.MESH


def tables(points):
    numbers = np.arange(points, dtype=np.float64) + 1.0
    sine = np.sqrt(2.0 / (points + 1.0)) * np.sin(
        np.pi * numbers[:, None] * numbers[None, :] / (points + 1.0)
    )
    eigen = 2.0 - 2.0 * np.cos(np.pi * numbers / (points + 1.0))
    sine = sine.astype(np.float32)
    high = sine.astype(jnp.bfloat16)
    low = (sine - high.astype(np.float32)).astype(jnp.bfloat16)
    half = np.concatenate([high, low], axis=1)
    right = np.concatenate([half, half], axis=0)
    diagonal = 2.0 + lateral * (eigen[:, None] + eigen[None, :]) + screening
    return right, np.ascontiguousarray(right.T), diagonal.astype(np.float32)


def split(value):
    high = value.astype(jnp.bfloat16)
    low = (value - high.astype(jnp.float32)).astype(jnp.bfloat16)
    return high, low


def plane_pair(first, second, right, left):
    points = first.shape[0]
    high, low = split(jnp.concatenate([first, second], axis=0))
    both = jnp.dot(
        jnp.concatenate([high, low], axis=1), right, preferred_element_type=jnp.float32
    )
    rows = both[:, :points] + both[:, points:]
    high, low = split(rows)
    stacked = jnp.concatenate(
        [
            jnp.concatenate([high[:points], high[points:]], axis=1),
            jnp.concatenate([low[:points], low[points:]], axis=1),
        ],
        axis=0,
    )
    both = jnp.dot(left, stacked, preferred_element_type=jnp.float32)
    result = both[:points] + both[points:]
    return result[:, :points], result[:, points:]


def chunks_of(planes):
    return max(1, min(4, planes // 4))


def kernel(
    bands, slabs,
    orbitals_hbm, occupation_hbm, assignment_hbm, live_hbm, right_hbm, left_hbm, diagonal_hbm,
    out, returned,
    occupation, assignment, live, right_ref, left_ref, diagonal_ref,
    orbitals, visitors, visit_sum, spectra, ends_in, ends_out,
    faces, face_out, edges, edge_out, merged,
    pivots, reach, coefs, ratios, bounds, weight_out, weight_in,
    send_orb, recv_orb, send_weight, recv_weight, send_back, recv_back,
    send_end, recv_end, send_face, recv_face, send_edge, recv_edge,
    load_sem,
):
    members, planes, points, _ = orbitals_hbm.shape
    pairs = members * members
    chunks = chunks_of(planes)
    depth = planes // chunks
    load = pltpu.make_async_copy(orbitals_hbm, orbitals, load_sem.at[0])
    tables_in = [
        pltpu.make_async_copy(source, target, load_sem.at[n + 1])
        for n, (source, target) in enumerate((
            (occupation_hbm, occupation), (assignment_hbm, assignment), (live_hbm, live),
            (diagonal_hbm, diagonal_ref), (right_hbm, right_ref), (left_hbm, left_ref),
        ))
    ]
    band = lax.axis_index("band")
    slab = lax.axis_index("slab")
    above = lax.rem(band + 1, bands)
    below = lax.rem(band + bands - 1, bands)
    side = lax.rem(slab, 2)
    partner = slab + 1 - 2 * side
    duo, duos = slab // 2, slabs // 2
    half = points // 2
    mine = pl.ds(pl.multiple_of(side * half, half), half)
    other = pl.ds(pl.multiple_of((1 - side) * half, half), half)

    barrier = pltpu.get_barrier_semaphore()
    for neighbour in (above, below):
        pl.semaphore_signal(barrier, inc=1, device_id=(neighbour, slab), device_id_type=MESH)
    pl.semaphore_signal(barrier, inc=1, device_id=(band, partner), device_id_type=MESH)

    @pl.loop(0, duos)
    def _(d):
        @pl.when(d != duo)
        def _():
            pl.semaphore_signal(
                barrier, inc=1, device_id=(band, 2 * d + side), device_id_type=MESH
            )

    for copy in tables_in:
        copy.start()
    load.start()
    tables_in[0].wait()
    tables_in[1].wait()
    weights = [occupation[assignment[k]] for k in range(members)]
    for k in range(members):
        weight_out[k] = jnp.full(weight_out.shape[1:], weights[k], jnp.float32)
    pl.semaphore_wait(barrier, 2 + duos)

    def remote(source, target, sent, landed, device):
        return pltpu.make_async_remote_copy(
            src_ref=source, dst_ref=target, send_sem=sent, recv_sem=landed,
            device_id=device, device_id_type=MESH,
        )

    def orb_copy(k, c):
        span = pl.ds(c * depth, depth)
        return remote(
            orbitals_hbm.at[k, span], visitors.at[k, span],
            send_orb.at[k, c], recv_orb.at[k, c], (above, slab),
        )

    def back_copy(k, part):
        span = pl.ds(part * (planes // 2), planes // 2)
        return remote(
            visit_sum.at[k, span], returned.at[k, span],
            send_back.at[k, part], recv_back.at[k, part], (below, slab),
        )

    def end_copy(p, d):
        way = (d < duo).astype(jnp.int32)
        return remote(
            ends_out.at[p, way], ends_in.at[p, duo], send_end.at[p, d], recv_end.at[p, duo],
            (band, 2 * d + side),
        )

    def end_arrival(p, d):
        return remote(
            ends_out.at[p, 0], ends_in.at[p, d], send_end.at[p, d], recv_end.at[p, d],
            (band, 2 * d + side),
        )

    def face_copy(p):
        return remote(face_out.at[p], faces.at[p, side], send_face.at[p], recv_face.at[p], (band, partner))

    def edge_copy(p):
        return remote(edge_out.at[p], edges.at[p, side], send_edge.at[p], recv_edge.at[p], (band, partner))

    weight_copy = remote(weight_out, weight_in, send_weight, recv_weight, (above, slab))
    weight_copy.start()
    for k in range(members):
        for c in range(chunks):
            orb_copy(k, c).start()
    for copy in tables_in[2:]:
        copy.wait()

    diagonal = diagonal_ref[...]
    pivot = 1.0 / diagonal
    pivots[0] = pivot
    for z in range(1, planes):
        pivot = 1.0 / (diagonal - pivot)
        pivots[z] = pivot
    response = pivot
    reach[planes - 1] = response
    for z in range(planes - 2, -1, -1):
        response = response * pivots[z]
        reach[z] = response
    near, far = reach[planes - 1, mine, :], reach[0, mine, :]
    inner = 1.0 / (1.0 - near * near)
    near_two = near + far * far * near * inner
    far_two = far * far * inner

    def closing(d, value):
        gap = 1.0 - value * near_two
        ratios[d] = far_two / gap
        coefs[0] = jnp.where(d == duo, value, coefs[0])
        coefs[1] = jnp.where(d == duos - 1 - duo, value, coefs[1])
        return near_two + far_two * far_two * value / gap

    coefs[0] = jnp.zeros_like(near)
    coefs[1] = jnp.zeros_like(near)
    lax.fori_loop(0, duos, closing, jnp.zeros_like(near))
    close_left, close_right = coefs[0], coefs[1]
    gap_left = 1.0 - close_left * near_two
    gap_right = 1.0 - close_right * near_two
    scale = 1.0 / (gap_left * gap_right - close_left * close_right * far_two * far_two)
    coefs[2] = far_two / gap_left
    coefs[3] = far_two / gap_right
    coefs[4] = gap_right * scale
    coefs[5] = close_left * far_two * scale
    coefs[6] = gap_left * scale
    coefs[7] = close_right * far_two * scale
    coefs[8] = inner
    coefs[9] = near * inner
    coefs[10] = far

    @pl.loop(0, members)
    def _(k):
        @pl.loop(0, planes)
        def _(z):
            zero = jnp.zeros((points, points), jnp.float32)
            out[k, z] = zero
            visit_sum[k, z] = zero

    weight_copy.wait()
    load.wait()

    def forward(k, c):
        orb_copy(k, c).wait()

        for i in range(members):
            p = k * members + i
            carry = spectra[p, c * depth - 1] if c else jnp.zeros((points, points), jnp.float32)
            for z in range(c * depth, (c + 1) * depth, 2):
                one, two = plane_pair(
                    orbitals[i, z] * visitors[k, z],
                    orbitals[i, z + 1] * visitors[k, z + 1],
                    right_ref[...], left_ref[...],
                )
                one = (one + carry) * pivots[z]
                spectra[p, z] = one
                carry = (two + one) * pivots[z + 1]
                spectra[p, z + 1] = carry

    def backward(p):
        def back(h, value):
            z = planes - 2 - h
            value = spectra[p, z] + pivots[z] * value
            spectra[p, z] = value
            return value

        lax.fori_loop(0, planes - 1, back, spectra[p, planes - 1], unroll=min(3, planes - 1))
        for n, z in enumerate((0, planes - 1)):
            face_out[p, n] = spectra[p, z, other, :]
            faces[p, side, n] = spectra[p, z, mine, :]
        face_copy(p).start()

    def merge(p):
        face_copy(p).wait_recv()
        head, tail = faces[p, 0, 1], faces[p, 1, 0]
        lower_end = faces[p, 0, 0] + coefs[10] * (coefs[8] * tail + coefs[9] * head)
        upper_end = faces[p, 1, 1] + coefs[10] * (coefs[8] * head + coefs[9] * tail)
        merged[p, 0], merged[p, 1] = lower_end, upper_end
        ends_out[p, 0] = upper_end + coefs[2] * (coefs[0] * lower_end)
        ends_out[p, 1] = lower_end + coefs[3] * (coefs[1] * upper_end)

        @pl.loop(0, duos)
        def _(d):
            @pl.when(d != duo)
            def _():
                end_copy(p, d).start()

    def finish(p):
        @pl.loop(0, duos)
        def _(d):
            @pl.when(d != duo)
            def _():
                end_arrival(p, d).wait_recv()

        nothing = jnp.zeros((half, points), jnp.float32)
        below_end = lax.fori_loop(
            0, duo, lambda d, value: ends_in[p, d] + ratios[d] * value, nothing
        )
        above_end = lax.fori_loop(
            0, duos - 1 - duo,
            lambda d, value: ends_in[p, duos - 1 - d] + ratios[d] * value, nothing,
        )
        from_left = below_end + coefs[0] * merged[p, 0]
        from_right = above_end + coefs[1] * merged[p, 1]
        beyond_left = coefs[4] * from_left + coefs[5] * from_right
        beyond_right = coefs[6] * from_right + coefs[7] * from_left
        head = faces[p, 0, 1] + coefs[10] * beyond_left
        tail = faces[p, 1, 0] + coefs[10] * beyond_right
        inner_left = coefs[8] * head + coefs[9] * tail
        inner_right = coefs[8] * tail + coefs[9] * head
        lower = side == 0
        edges[p, side, 0] = jnp.where(lower, beyond_left, inner_left)
        edges[p, side, 1] = jnp.where(lower, inner_right, beyond_right)
        edge_out[p, 0] = jnp.where(lower, inner_left, beyond_left)
        edge_out[p, 1] = jnp.where(lower, beyond_right, inner_right)
        edge_copy(p).start()

    def inverse(p):
        j, i = p // members, lax.rem(p, members)
        edge_copy(p).wait_recv()
        for n in range(2):
            bounds[n] = jnp.concatenate([edges[p, 0, n], edges[p, 1, n]], axis=0)
        planned = live[i, below * members + j].astype(jnp.float32)
        own_weight = occupation[assignment[i]]
        own_factor = weight_in[j, 0:1, :] * (-planned)
        visit_factor = -(planned * own_weight)

        for part in range(2):
            @pl.loop(part * (planes // 4), (part + 1) * (planes // 4), unroll=min(4, planes // 4))
            def _(h):
                z = 2 * h
                one = spectra[p, z] + reach[planes - 1 - z] * bounds[0] + reach[z] * bounds[1]
                two = spectra[p, z + 1] + reach[planes - 2 - z] * bounds[0] + reach[z + 1] * bounds[1]
                one, two = plane_pair(one, two, right_ref[...], left_ref[...])
                for y, value in ((z, one), (z + 1, two)):
                    out[i, y] += own_factor * (value * visitors[j, y])
                    visit_sum[j, y] += visit_factor * (value * orbitals[i, y])

            @pl.when(i == members - 1)
            def _():
                back_copy(j, part).start()

    def each(k, stage):
        @pl.loop(0, members)
        def _(i):
            stage(k * members + i)

    @pl.loop(0, members + 2)
    def _(k):
        entering = k < members
        meeting = jnp.logical_and(k >= 1, k <= members)
        leaving = k >= 2

        @pl.when(entering)
        def _():
            forward(k, 0)

        @pl.loop(0, members)
        def _(i):
            @pl.when(leaving)
            def _():
                inverse((k - 2) * members + i)

            @pl.when(jnp.logical_and(meeting, i == 0))
            def _():
                each(k - 1, merge)

        @pl.when(entering)
        def _():
            for c in range(1, chunks):
                forward(k, c)
            each(k, backward)

        @pl.when(meeting)
        def _():
            each(k - 1, finish)

    for k in range(members):
        for part in range(2):
            back_copy(k, part).wait_send()

    @pl.loop(0, pairs)
    def _(p):
        face_copy(p).wait_send()
        edge_copy(p).wait_send()

        @pl.loop(0, duos)
        def _(d):
            @pl.when(d != duo)
            def _():
                end_arrival(p, d).wait_send()

    for k in range(members):
        for part in range(2):
            back_copy(k, part).wait_recv()


def local(bands, slabs, orbitals, occupation, assignment, pair_live):
    members, planes, points, _ = orbitals.shape
    pairs = members * members
    chunks = chunks_of(planes)
    right, left, diagonal = tables(points)
    hbm = pl.BlockSpec(memory_space=pltpu.HBM)
    result = pltpu.VMEM(orbitals.shape, jnp.float32)
    arguments = (
        orbitals, occupation, assignment, pair_live,
        jnp.asarray(right), jnp.asarray(left), jnp.asarray(diagonal),
    )
    block = pltpu.VMEM((members, planes, points, points), jnp.float32)
    twice = pltpu.VMEM((pairs, 2, points // 2, points), jnp.float32)
    quad = pltpu.VMEM((pairs, 2, 2, points // 2, points), jnp.float32)
    column = pltpu.VMEM((planes, points, points), jnp.float32)
    dma = pltpu.SemaphoreType.DMA
    own, returned = pl.pallas_call(
        functools.partial(kernel, bands, slabs),
        out_shape=[result, result],
        in_specs=[hbm] * 7,
        out_specs=[pl.BlockSpec(memory_space=pltpu.VMEM)] * 2,
        scratch_shapes=[
            pltpu.SMEM(occupation.shape, occupation.dtype),
            pltpu.SMEM(assignment.shape, assignment.dtype),
            pltpu.SMEM(pair_live.shape, pair_live.dtype),
            pltpu.VMEM(right.shape, right.dtype),
            pltpu.VMEM(left.shape, left.dtype),
            pltpu.VMEM(diagonal.shape, diagonal.dtype),
            block, block, block,
            pltpu.VMEM((pairs, planes, points, points), jnp.float32),
            pltpu.VMEM((pairs, slabs // 2, points // 2, points), jnp.float32), twice,
            quad, twice, quad, twice, twice,
            column, column,
            pltpu.VMEM((11, points // 2, points), jnp.float32),
            pltpu.VMEM((slabs // 2, points // 2, points), jnp.float32),
            pltpu.VMEM((2, points, points), jnp.float32),
            pltpu.VMEM((members, 8, points), jnp.float32),
            pltpu.VMEM((members, 8, points), jnp.float32),
            dma((members, chunks)), dma((members, chunks)), dma, dma, dma((members, 2)), dma((members, 2)),
            dma((pairs, slabs // 2)), dma((pairs, slabs // 2)),
            *[dma((pairs,)) for _ in range(4)],
            dma((7,)),
        ],
        compiler_params=pltpu.CompilerParams(
            collective_id=0, has_side_effects=True, vmem_limit_bytes=40000 * 1024
        ),
    )(*[pltpu.with_memory_space_constraint(a, pltpu.HBM) for a in arguments])
    return own + returned


def solution(mesh):
    placed = (P("band", "slab", None, None), P(), P("band"), P("band", None))
    return jax.shard_map(
        functools.partial(local, mesh.shape["band"], mesh.shape["slab"]),
        mesh=mesh, in_specs=placed, out_specs=P("band", "slab", None, None), check_vma=False,
    )
```

```python
import functools

import jax
import jax.numpy as jnp
import numpy as np
from jax import lax
from jax.experimental import pallas as pl
from jax.experimental.pallas import tpu as pltpu
from jax.sharding import PartitionSpec as P

screening = 0.01
lateral = 0.01
MESH = pl.DeviceIdType.MESH


def tables(points):
    numbers = np.arange(points, dtype=np.float64) + 1.0
    sine = np.sqrt(2.0 / (points + 1.0)) * np.sin(
        np.pi * numbers[:, None] * numbers[None, :] / (points + 1.0)
    )
    eigen = 2.0 - 2.0 * np.cos(np.pi * numbers / (points + 1.0))
    sine = sine.astype(np.float32)
    high = sine.astype(jnp.bfloat16)
    low = (sine - high.astype(np.float32)).astype(jnp.bfloat16)
    half = np.concatenate([high, low], axis=1)
    right = np.concatenate([half, half], axis=0)
    diagonal = 2.0 + lateral * (eigen[:, None] + eigen[None, :]) + screening
    return right, np.ascontiguousarray(right.T), diagonal.astype(np.float32)


def split(value):
    high = value.astype(jnp.bfloat16)
    low = (value - high.astype(jnp.float32)).astype(jnp.bfloat16)
    return high, low


def plane_pair(first, second, right, left):
    points = first.shape[0]
    high, low = split(jnp.concatenate([first, second], axis=0))
    both = jnp.dot(
        jnp.concatenate([high, low], axis=1), right, preferred_element_type=jnp.float32
    )
    rows = both[:, :points] + both[:, points:]
    high, low = split(rows)
    stacked = jnp.concatenate(
        [
            jnp.concatenate([high[:points], high[points:]], axis=1),
            jnp.concatenate([low[:points], low[points:]], axis=1),
        ],
        axis=0,
    )
    both = jnp.dot(left, stacked, preferred_element_type=jnp.float32)
    result = both[:points] + both[points:]
    return result[:, :points], result[:, points:]


def chunks_of(planes):
    return max(1, min(4, planes // 4))


def kernel(
    bands, slabs,
    orbitals_hbm, occupation_hbm, assignment_hbm, live_hbm, right_hbm, left_hbm, diagonal_hbm,
    out,
    occupation, assignment, live, right_ref, left_ref, diagonal_ref,
    orbitals, visitors, visit_sum, returned, spectra, ends_in, ends_out,
    faces, face_out, edges, edge_out, merged,
    pivots, reach, coefs, ratios, bounds, weight_out, weight_in,
    send_orb, recv_orb, send_weight, recv_weight, send_back, recv_back,
    send_end, recv_end, send_face, recv_face, send_edge, recv_edge,
    load_sem,
):
    members, planes, points, _ = orbitals_hbm.shape
    pairs = members * members
    chunks = chunks_of(planes)
    depth = planes // chunks
    early = chunks // 2
    parts, share = chunks, depth
    load = pltpu.make_async_copy(orbitals_hbm, orbitals, load_sem.at[0])
    tables_in = [
        pltpu.make_async_copy(source, target, load_sem.at[n + 1])
        for n, (source, target) in enumerate((
            (occupation_hbm, occupation), (assignment_hbm, assignment), (live_hbm, live),
            (diagonal_hbm, diagonal_ref), (right_hbm, right_ref), (left_hbm, left_ref),
        ))
    ]
    band = lax.axis_index("band")
    slab = lax.axis_index("slab")
    above = lax.rem(band + 1, bands)
    below = lax.rem(band + bands - 1, bands)
    side = lax.rem(slab, 2)
    partner = slab + 1 - 2 * side
    duo, duos = slab // 2, slabs // 2
    half = points // 2
    mine = pl.ds(pl.multiple_of(side * half, half), half)
    other = pl.ds(pl.multiple_of((1 - side) * half, half), half)

    barrier = pltpu.get_barrier_semaphore()
    for neighbour in (above, below):
        pl.semaphore_signal(barrier, inc=1, device_id=(neighbour, slab), device_id_type=MESH)
    pl.semaphore_signal(barrier, inc=1, device_id=(band, partner), device_id_type=MESH)

    @pl.loop(0, duos)
    def _(d):
        @pl.when(d != duo)
        def _():
            pl.semaphore_signal(
                barrier, inc=1, device_id=(band, 2 * d + side), device_id_type=MESH
            )

    for copy in tables_in:
        copy.start()
    load.start()
    tables_in[0].wait()
    tables_in[1].wait()
    weights = [occupation[assignment[k]] for k in range(members)]
    for k in range(members):
        weight_out[k] = jnp.full(weight_out.shape[1:], weights[k], jnp.float32)
    pl.semaphore_wait(barrier, 2 + duos)

    def remote(source, target, sent, landed, device):
        return pltpu.make_async_remote_copy(
            src_ref=source, dst_ref=target, send_sem=sent, recv_sem=landed,
            device_id=device, device_id_type=MESH,
        )

    def orb_copy(k, c):
        span = pl.ds(c * depth, depth)
        return remote(
            orbitals_hbm.at[k, span], visitors.at[k, span],
            send_orb.at[k, c], recv_orb.at[k, c], (above, slab),
        )

    def back_copy(k, part):
        span = pl.ds(part * share, share)
        return remote(
            visit_sum.at[k, span], returned.at[k, span],
            send_back.at[k, part], recv_back.at[k, part], (below, slab),
        )

    def end_copy(p, d):
        way = (d < duo).astype(jnp.int32)
        return remote(
            ends_out.at[p, way], ends_in.at[p, duo], send_end.at[p, d], recv_end.at[p, duo],
            (band, 2 * d + side),
        )

    def end_arrival(p, d):
        return remote(
            ends_out.at[p, 0], ends_in.at[p, d], send_end.at[p, d], recv_end.at[p, d],
            (band, 2 * d + side),
        )

    def face_copy(p):
        return remote(face_out.at[p], faces.at[p, side], send_face.at[p], recv_face.at[p], (band, partner))

    def edge_copy(p):
        return remote(edge_out.at[p], edges.at[p, side], send_edge.at[p], recv_edge.at[p], (band, partner))

    weight_copy = remote(weight_out, weight_in, send_weight, recv_weight, (above, slab))
    weight_copy.start()
    for k in range(members):
        for c in range(chunks):
            orb_copy(k, c).start()
    for copy in tables_in[2:]:
        copy.wait()

    diagonal = diagonal_ref[...]
    pivot = 1.0 / diagonal
    pivots[0] = pivot
    for z in range(1, planes):
        pivot = 1.0 / (diagonal - pivot)
        pivots[z] = pivot
    response = pivot
    reach[planes - 1] = response
    for z in range(planes - 2, -1, -1):
        response = response * pivots[z]
        reach[z] = response
    near, far = reach[planes - 1, mine, :], reach[0, mine, :]
    inner = 1.0 / (1.0 - near * near)
    near_two = near + far * far * near * inner
    far_two = far * far * inner

    def closing(d, value):
        gap = 1.0 - value * near_two
        ratios[d] = far_two / gap
        coefs[0] = jnp.where(d == duo, value, coefs[0])
        coefs[1] = jnp.where(d == duos - 1 - duo, value, coefs[1])
        return near_two + far_two * far_two * value / gap

    coefs[0] = jnp.zeros_like(near)
    coefs[1] = jnp.zeros_like(near)
    lax.fori_loop(0, duos, closing, jnp.zeros_like(near))
    close_left, close_right = coefs[0], coefs[1]
    gap_left = 1.0 - close_left * near_two
    gap_right = 1.0 - close_right * near_two
    scale = 1.0 / (gap_left * gap_right - close_left * close_right * far_two * far_two)
    coefs[2] = far_two / gap_left
    coefs[3] = far_two / gap_right
    coefs[4] = gap_right * scale
    coefs[5] = close_left * far_two * scale
    coefs[6] = gap_left * scale
    coefs[7] = close_right * far_two * scale
    coefs[8] = inner
    coefs[9] = near * inner
    coefs[10] = far

    @pl.loop(0, members)
    def _(k):
        @pl.loop(0, planes)
        def _(z):
            zero = jnp.zeros((points, points), jnp.float32)
            out[k, z] = zero

    weight_copy.wait()
    load.wait()

    def forward(k, c):
        orb_copy(k, c).wait_recv()

        for i in range(members):
            p = k * members + i
            carry = spectra[p, c * depth - 1] if c else jnp.zeros((points, points), jnp.float32)
            for z in range(c * depth, (c + 1) * depth, 2):
                one, two = plane_pair(
                    orbitals[i, z] * visitors[k, z],
                    orbitals[i, z + 1] * visitors[k, z + 1],
                    right_ref[...], left_ref[...],
                )
                one = (one + carry) * pivots[z]
                spectra[p, z] = one
                carry = (two + one) * pivots[z + 1]
                spectra[p, z + 1] = carry

    def backward(p):
        def back(h, value):
            z = planes - 2 - h
            value = spectra[p, z] + pivots[z] * value
            spectra[p, z] = value
            return value

        lax.fori_loop(0, planes - 1, back, spectra[p, planes - 1], unroll=min(3, planes - 1))
        for n, z in enumerate((0, planes - 1)):
            face_out[p, n] = spectra[p, z, other, :]
            faces[p, side, n] = spectra[p, z, mine, :]
        face_copy(p).start()

    def merge(p):
        face_copy(p).wait_recv()
        head, tail = faces[p, 0, 1], faces[p, 1, 0]
        lower_end = faces[p, 0, 0] + coefs[10] * (coefs[8] * tail + coefs[9] * head)
        upper_end = faces[p, 1, 1] + coefs[10] * (coefs[8] * head + coefs[9] * tail)
        merged[p, 0], merged[p, 1] = lower_end, upper_end
        ends_out[p, 0] = upper_end + coefs[2] * (coefs[0] * lower_end)
        ends_out[p, 1] = lower_end + coefs[3] * (coefs[1] * upper_end)

        @pl.loop(0, duos)
        def _(d):
            @pl.when(d != duo)
            def _():
                end_copy(p, d).start()

    def finish(p):
        @pl.loop(0, duos)
        def _(d):
            @pl.when(d != duo)
            def _():
                end_arrival(p, d).wait_recv()

        nothing = jnp.zeros((half, points), jnp.float32)
        below_end = lax.fori_loop(
            0, duo, lambda d, value: ends_in[p, d] + ratios[d] * value, nothing
        )
        above_end = lax.fori_loop(
            0, duos - 1 - duo,
            lambda d, value: ends_in[p, duos - 1 - d] + ratios[d] * value, nothing,
        )
        from_left = below_end + coefs[0] * merged[p, 0]
        from_right = above_end + coefs[1] * merged[p, 1]
        beyond_left = coefs[4] * from_left + coefs[5] * from_right
        beyond_right = coefs[6] * from_right + coefs[7] * from_left
        head = faces[p, 0, 1] + coefs[10] * beyond_left
        tail = faces[p, 1, 0] + coefs[10] * beyond_right
        inner_left = coefs[8] * head + coefs[9] * tail
        inner_right = coefs[8] * tail + coefs[9] * head
        lower = side == 0
        edges[p, side, 0] = jnp.where(lower, beyond_left, inner_left)
        edges[p, side, 1] = jnp.where(lower, inner_right, beyond_right)
        edge_out[p, 0] = jnp.where(lower, inner_left, beyond_left)
        edge_out[p, 1] = jnp.where(lower, beyond_right, inner_right)
        edge_copy(p).start()

    def inverse(k):
        own_factors, visit_factors = [], []
        for i in range(members):
            p = k * members + i
            edge_copy(p).wait_recv()
            for n in range(2):
                bounds[i, n] = jnp.concatenate([edges[p, 0, n], edges[p, 1, n]], axis=0)
            planned = live[i, below * members + k].astype(jnp.float32)
            own_factors.append(weight_in[k, 0:1, :] * (-planned))
            visit_factors.append(-(planned * occupation[assignment[i]]))

        @pl.loop(0, parts)
        def _(part):
            for h in range(share // 2):
                z = part * share + 2 * h
                sums = [None, None]
                for i in range(members):
                    p = k * members + i
                    fields = [
                        spectra[p, z + n] + reach[planes - 1 - n - z] * bounds[i, 0]
                        + reach[z + n] * bounds[i, 1]
                        for n in range(2)
                    ]
                    fields = plane_pair(*fields, right_ref[...], left_ref[...])
                    for n, value in enumerate(fields):
                        out[i, z + n] += own_factors[i] * (value * visitors[k, z + n])
                        term = visit_factors[i] * (value * orbitals[i, z + n])
                        sums[n] = term if sums[n] is None else sums[n] + term
                for n in range(2):
                    visit_sum[k, z + n] = sums[n]
            back_copy(k, part).start()

    def each(k, stage):
        @pl.loop(0, members)
        def _(i):
            stage(k * members + i)

    @pl.loop(0, members + 2)
    def _(k):
        entering = k < members
        meeting = jnp.logical_and(k >= 1, k <= members)
        leaving = k >= 2

        @pl.when(entering)
        def _():
            for c in range(early):
                forward(k, c)

        @pl.when(meeting)
        def _():
            each(k - 1, merge)

        @pl.when(leaving)
        def _():
            inverse(k - 2)

        @pl.when(entering)
        def _():
            for c in range(early, chunks):
                forward(k, c)
            each(k, backward)

        @pl.when(meeting)
        def _():
            each(k - 1, finish)


    @pl.loop(0, pairs)
    def _(p):
        face_copy(p).wait_send()
        edge_copy(p).wait_send()

        @pl.loop(0, duos)
        def _(d):
            @pl.when(d != duo)
            def _():
                end_arrival(p, d).wait_send()

    @pl.loop(0, members)
    def _(k):
        @pl.loop(0, parts)
        def _(part):
            orb_copy(k, part).wait_send()
            back_copy(k, part).wait()

            @pl.loop(0, share, unroll=True)
            def _(n):
                z = part * share + n
                out[k, z] += returned[k, z]


def local(bands, slabs, orbitals, occupation, assignment, pair_live):
    members, planes, points, _ = orbitals.shape
    pairs = members * members
    chunks = chunks_of(planes)
    right, left, diagonal = tables(points)
    hbm = pl.BlockSpec(memory_space=pltpu.HBM)
    arguments = (
        orbitals, occupation, assignment, pair_live,
        jnp.asarray(right), jnp.asarray(left), jnp.asarray(diagonal),
    )
    block = pltpu.VMEM((members, planes, points, points), jnp.float32)
    twice = pltpu.VMEM((pairs, 2, points // 2, points), jnp.float32)
    quad = pltpu.VMEM((pairs, 2, 2, points // 2, points), jnp.float32)
    column = pltpu.VMEM((planes, points, points), jnp.float32)
    dma = pltpu.SemaphoreType.DMA
    return pl.pallas_call(
        functools.partial(kernel, bands, slabs),
        out_shape=pltpu.VMEM(orbitals.shape, jnp.float32),
        in_specs=[hbm] * 7,
        out_specs=pl.BlockSpec(memory_space=pltpu.VMEM),
        scratch_shapes=[
            pltpu.SMEM(occupation.shape, occupation.dtype),
            pltpu.SMEM(assignment.shape, assignment.dtype),
            pltpu.SMEM(pair_live.shape, pair_live.dtype),
            pltpu.VMEM(right.shape, right.dtype),
            pltpu.VMEM(left.shape, left.dtype),
            pltpu.VMEM(diagonal.shape, diagonal.dtype),
            block, block, block, block,
            pltpu.VMEM((pairs, planes, points, points), jnp.float32),
            pltpu.VMEM((pairs, slabs // 2, points // 2, points), jnp.float32), twice,
            quad, twice, quad, twice, twice,
            column, column,
            pltpu.VMEM((11, points // 2, points), jnp.float32),
            pltpu.VMEM((slabs // 2, points // 2, points), jnp.float32),
            pltpu.VMEM((members, 2, points, points), jnp.float32),
            pltpu.VMEM((members, 8, points), jnp.float32),
            pltpu.VMEM((members, 8, points), jnp.float32),
            dma((members, chunks)), dma((members, chunks)), dma, dma, dma((members, chunks)), dma((members, chunks)),
            dma((pairs, slabs // 2)), dma((pairs, slabs // 2)),
            *[dma((pairs,)) for _ in range(4)],
            dma((7,)),
        ],
        compiler_params=pltpu.CompilerParams(
            collective_id=0, has_side_effects=True, vmem_limit_bytes=40000 * 1024
        ),
    )(*[pltpu.with_memory_space_constraint(a, pltpu.HBM) for a in arguments])


def solution(mesh):
    placed = (P("band", "slab", None, None), P(), P("band"), P("band", None))
    return jax.shard_map(
        functools.partial(local, mesh.shape["band"], mesh.shape["slab"]),
        mesh=mesh, in_specs=placed, out_specs=P("band", "slab", None, None), check_vma=False,
    )
```

```python
import functools

import jax
import jax.numpy as jnp
import numpy as np
from jax import lax
from jax.experimental import pallas as pl
from jax.experimental.pallas import tpu as pltpu
from jax.sharding import PartitionSpec as P

screening = 0.01
lateral = 0.01
MESH = pl.DeviceIdType.MESH


def tables(points):
    numbers = np.arange(points, dtype=np.float64) + 1.0
    sine = np.sqrt(2.0 / (points + 1.0)) * np.sin(
        np.pi * numbers[:, None] * numbers[None, :] / (points + 1.0)
    )
    eigen = 2.0 - 2.0 * np.cos(np.pi * numbers / (points + 1.0))
    sine = sine.astype(np.float32)
    high = sine.astype(jnp.bfloat16)
    low = (sine - high.astype(np.float32)).astype(jnp.bfloat16)
    half = np.concatenate([high, low], axis=1)
    right = np.concatenate([half, half], axis=0)
    diagonal = 2.0 + lateral * (eigen[:, None] + eigen[None, :]) + screening
    return right, np.ascontiguousarray(right.T), diagonal.astype(np.float32)


def split(value):
    high = value.astype(jnp.bfloat16)
    low = (value - high.astype(jnp.float32)).astype(jnp.bfloat16)
    return high, low


def plane_pair(first, second, right, left):
    points = first.shape[0]
    high, low = split(jnp.concatenate([first, second], axis=0))
    both = jnp.dot(
        jnp.concatenate([high, low], axis=1), right, preferred_element_type=jnp.float32
    )
    rows = both[:, :points] + both[:, points:]
    high, low = split(rows)
    stacked = jnp.concatenate(
        [
            jnp.concatenate([high[:points], high[points:]], axis=1),
            jnp.concatenate([low[:points], low[points:]], axis=1),
        ],
        axis=0,
    )
    both = jnp.dot(left, stacked, preferred_element_type=jnp.float32)
    result = both[:points] + both[points:]
    return result[:, :points], result[:, points:]


def chunks_of(planes):
    return max(1, min(4, planes // 4))


def kernel(
    bands, slabs,
    orbitals_hbm, occupation_hbm, assignment_hbm, live_hbm, right_hbm, left_hbm, diagonal_hbm,
    out,
    occupation, assignment, live, right_ref, left_ref, diagonal_ref,
    orbitals, visitors, visit_sum, returned, spectra, ends_in, ends_out,
    faces, face_out, edges, edge_out, merged,
    pivots, reach, coefs, ratios, bounds, weight_out, weight_in,
    send_orb, recv_orb, send_weight, recv_weight, send_back, recv_back,
    send_end, recv_end, send_face, recv_face, send_edge, recv_edge,
    load_sem, answer_sem, gather_sem,
):
    members, planes, points, _ = orbitals_hbm.shape
    pairs = members * members
    chunks = chunks_of(planes)
    depth = planes // chunks
    early = chunks // 2
    parts, share = chunks, depth
    load = pltpu.make_async_copy(orbitals_hbm, orbitals, load_sem.at[0])
    tables_in = [
        pltpu.make_async_copy(source, target, load_sem.at[n + 1])
        for n, (source, target) in enumerate((
            (occupation_hbm, occupation), (assignment_hbm, assignment), (live_hbm, live),
            (diagonal_hbm, diagonal_ref), (right_hbm, right_ref), (left_hbm, left_ref),
        ))
    ]
    band = lax.axis_index("band")
    slab = lax.axis_index("slab")
    above = lax.rem(band + 1, bands)
    below = lax.rem(band + bands - 1, bands)
    side = lax.rem(slab, 2)
    partner = slab + 1 - 2 * side
    duo, duos = slab // 2, slabs // 2
    half = points // 2
    mine = pl.ds(pl.multiple_of(side * half, half), half)
    other = pl.ds(pl.multiple_of((1 - side) * half, half), half)

    barrier = pltpu.get_barrier_semaphore()
    odd = lax.rem(band, 2) == 1
    even = jnp.logical_not(odd)

    def greet(semaphore, to_band, to_slab):
        pl.semaphore_signal(semaphore, inc=1, device_id=(to_band, to_slab), device_id_type=MESH)

    @pl.when(even)
    def _():
        greet(barrier, above, slab)
        greet(barrier, below, slab)

    for copy in tables_in:
        copy.start()
    load.start()
    tables_in[0].wait()
    tables_in[1].wait()
    weights = [occupation[assignment[k]] for k in range(members)]
    for k in range(members):
        weight_out[k] = jnp.full(weight_out.shape[1:], weights[k], jnp.float32)

    @pl.when(odd)
    def _():
        pl.semaphore_wait(barrier, 2)
        greet(answer_sem, above, slab)
        greet(answer_sem, below, slab)

    @pl.when(even)
    def _():
        pl.semaphore_wait(answer_sem, 2)
        greet(barrier, band, partner)

        @pl.loop(0, duos)
        def _(d):
            @pl.when(d != duo)
            def _():
                greet(barrier, band, 2 * d + side)

    def remote(source, target, sent, landed, device):
        return pltpu.make_async_remote_copy(
            src_ref=source, dst_ref=target, send_sem=sent, recv_sem=landed,
            device_id=device, device_id_type=MESH,
        )

    def orb_copy(k, c):
        span = pl.ds(c * depth, depth)
        return remote(
            orbitals_hbm.at[k, span], visitors.at[k, span],
            send_orb.at[k, c], recv_orb.at[k, c], (above, slab),
        )

    def back_copy(k, part):
        span = pl.ds(part * share, share)
        return remote(
            visit_sum.at[k, span], returned.at[k, span],
            send_back.at[k, part], recv_back.at[k, part], (below, slab),
        )

    def end_copy(p, d):
        way = (d < duo).astype(jnp.int32)
        return remote(
            ends_out.at[p, way], ends_in.at[p, duo], send_end.at[p, d], recv_end.at[p, duo],
            (band, 2 * d + side),
        )

    def end_arrival(p, d):
        return remote(
            ends_out.at[p, 0], ends_in.at[p, d], send_end.at[p, d], recv_end.at[p, d],
            (band, 2 * d + side),
        )

    def face_copy(p):
        return remote(face_out.at[p], faces.at[p, side], send_face.at[p], recv_face.at[p], (band, partner))

    def edge_copy(p):
        return remote(edge_out.at[p], edges.at[p, side], send_edge.at[p], recv_edge.at[p], (band, partner))

    weight_copy = remote(weight_out, weight_in, send_weight, recv_weight, (above, slab))
    weight_copy.start()
    for k in range(members):
        for c in range(chunks):
            orb_copy(k, c).start()
    for copy in tables_in[2:]:
        copy.wait()

    diagonal = diagonal_ref[...]
    pivot = 1.0 / diagonal
    pivots[0] = pivot
    for z in range(1, planes):
        pivot = 1.0 / (diagonal - pivot)
        pivots[z] = pivot
    response = pivot
    reach[planes - 1] = response
    for z in range(planes - 2, -1, -1):
        response = response * pivots[z]
        reach[z] = response
    near, far = reach[planes - 1, mine, :], reach[0, mine, :]
    inner = 1.0 / (1.0 - near * near)
    near_two = near + far * far * near * inner
    far_two = far * far * inner

    def closing(d, value):
        gap = 1.0 - value * near_two
        ratios[d] = far_two / gap
        coefs[0] = jnp.where(d == duo, value, coefs[0])
        coefs[1] = jnp.where(d == duos - 1 - duo, value, coefs[1])
        return near_two + far_two * far_two * value / gap

    coefs[0] = jnp.zeros_like(near)
    coefs[1] = jnp.zeros_like(near)
    lax.fori_loop(0, duos, closing, jnp.zeros_like(near))
    close_left, close_right = coefs[0], coefs[1]
    gap_left = 1.0 - close_left * near_two
    gap_right = 1.0 - close_right * near_two
    scale = 1.0 / (gap_left * gap_right - close_left * close_right * far_two * far_two)
    coefs[2] = far_two / gap_left
    coefs[3] = far_two / gap_right
    coefs[4] = gap_right * scale
    coefs[5] = close_left * far_two * scale
    coefs[6] = gap_left * scale
    coefs[7] = close_right * far_two * scale
    coefs[8] = inner
    coefs[9] = near * inner
    coefs[10] = far

    @pl.loop(0, members)
    def _(k):
        @pl.loop(0, planes)
        def _(z):
            zero = jnp.zeros((points, points), jnp.float32)
            out[k, z] = zero

    weight_copy.wait()
    load.wait()

    def forward(k, c):
        orb_copy(k, c).wait_recv()

        for i in range(members):
            p = k * members + i
            carry = spectra[p, c * depth - 1] if c else jnp.zeros((points, points), jnp.float32)
            for z in range(c * depth, (c + 1) * depth, 2):
                one, two = plane_pair(
                    orbitals[i, z] * visitors[k, z],
                    orbitals[i, z + 1] * visitors[k, z + 1],
                    right_ref[...], left_ref[...],
                )
                one = (one + carry) * pivots[z]
                spectra[p, z] = one
                carry = (two + one) * pivots[z + 1]
                spectra[p, z + 1] = carry

    def backward(p):
        def back(h, value):
            z = planes - 2 - h
            value = spectra[p, z] + pivots[z] * value
            spectra[p, z] = value
            return value

        lax.fori_loop(0, planes - 1, back, spectra[p, planes - 1], unroll=min(3, planes - 1))
        for n, z in enumerate((0, planes - 1)):
            face_out[p, n] = spectra[p, z, other, :]
            faces[p, side, n] = spectra[p, z, mine, :]
        face_copy(p).start()

    def merge(p):
        face_copy(p).wait_recv()
        head, tail = faces[p, 0, 1], faces[p, 1, 0]
        lower_end = faces[p, 0, 0] + coefs[10] * (coefs[8] * tail + coefs[9] * head)
        upper_end = faces[p, 1, 1] + coefs[10] * (coefs[8] * head + coefs[9] * tail)
        merged[p, 0], merged[p, 1] = lower_end, upper_end
        ends_out[p, 0] = upper_end + coefs[2] * (coefs[0] * lower_end)
        ends_out[p, 1] = lower_end + coefs[3] * (coefs[1] * upper_end)

        @pl.loop(0, duos)
        def _(d):
            @pl.when(d != duo)
            def _():
                end_copy(p, d).start()

    def finish(p):
        @pl.loop(0, duos)
        def _(d):
            @pl.when(d != duo)
            def _():
                end_arrival(p, d).wait_recv()

        nothing = jnp.zeros((half, points), jnp.float32)
        below_end = lax.fori_loop(
            0, duo, lambda d, value: ends_in[p, d] + ratios[d] * value, nothing
        )
        above_end = lax.fori_loop(
            0, duos - 1 - duo,
            lambda d, value: ends_in[p, duos - 1 - d] + ratios[d] * value, nothing,
        )
        from_left = below_end + coefs[0] * merged[p, 0]
        from_right = above_end + coefs[1] * merged[p, 1]
        beyond_left = coefs[4] * from_left + coefs[5] * from_right
        beyond_right = coefs[6] * from_right + coefs[7] * from_left
        head = faces[p, 0, 1] + coefs[10] * beyond_left
        tail = faces[p, 1, 0] + coefs[10] * beyond_right
        inner_left = coefs[8] * head + coefs[9] * tail
        inner_right = coefs[8] * tail + coefs[9] * head
        lower = side == 0
        edges[p, side, 0] = jnp.where(lower, beyond_left, inner_left)
        edges[p, side, 1] = jnp.where(lower, inner_right, beyond_right)
        edge_out[p, 0] = jnp.where(lower, inner_left, beyond_left)
        edge_out[p, 1] = jnp.where(lower, beyond_right, inner_right)
        edge_copy(p).start()

    def inverse(k):
        own_factors, visit_factors = [], []
        for i in range(members):
            p = k * members + i
            edge_copy(p).wait_recv()
            for n in range(2):
                bounds[i, n] = jnp.concatenate([edges[p, 0, n], edges[p, 1, n]], axis=0)
            planned = live[i, below * members + k].astype(jnp.float32)
            own_factors.append(weight_in[k, 0:1, :] * (-planned))
            visit_factors.append(-(planned * occupation[assignment[i]]))

        @pl.loop(0, parts)
        def _(part):
            for h in range(share // 2):
                z = part * share + 2 * h
                sums = [None, None]
                for i in range(members):
                    p = k * members + i
                    fields = [
                        spectra[p, z + n] + reach[planes - 1 - n - z] * bounds[i, 0]
                        + reach[z + n] * bounds[i, 1]
                        for n in range(2)
                    ]
                    fields = plane_pair(*fields, right_ref[...], left_ref[...])
                    for n, value in enumerate(fields):
                        out[i, z + n] += own_factors[i] * (value * visitors[k, z + n])
                        term = visit_factors[i] * (value * orbitals[i, z + n])
                        sums[n] = term if sums[n] is None else sums[n] + term
                for n in range(2):
                    visit_sum[k, z + n] = sums[n]
            back_copy(k, part).start()

    def each(k, stage):
        @pl.loop(0, members)
        def _(i):
            stage(k * members + i)

    @pl.loop(0, members + 2)
    def _(k):
        entering = k < members
        meeting = jnp.logical_and(k >= 1, k <= members)
        leaving = k >= 2

        @pl.when(entering)
        def _():
            for c in range(early):
                forward(k, c)

        @pl.when(meeting)
        def _():
            each(k - 1, merge)

        @pl.when(leaving)
        def _():
            inverse(k - 2)

        @pl.when(entering)
        def _():
            for c in range(early, chunks):
                forward(k, c)

            @pl.when(jnp.logical_and(even, k == 0))
            def _():
                pl.semaphore_wait(barrier, duos)
                greet(gather_sem, above, slab)

            @pl.when(jnp.logical_and(odd, k == 0))
            def _():
                pl.semaphore_wait(gather_sem, 1)

            each(k, backward)

        @pl.when(meeting)
        def _():
            each(k - 1, finish)


    @pl.loop(0, pairs)
    def _(p):
        face_copy(p).wait_send()
        edge_copy(p).wait_send()

        @pl.loop(0, duos)
        def _(d):
            @pl.when(d != duo)
            def _():
                end_arrival(p, d).wait_send()

    @pl.loop(0, members)
    def _(k):
        @pl.loop(0, parts)
        def _(part):
            orb_copy(k, part).wait_send()
            back_copy(k, part).wait()

            @pl.loop(0, share, unroll=True)
            def _(n):
                z = part * share + n
                out[k, z] += returned[k, z]


def local(bands, slabs, orbitals, occupation, assignment, pair_live):
    members, planes, points, _ = orbitals.shape
    pairs = members * members
    chunks = chunks_of(planes)
    right, left, diagonal = tables(points)
    hbm = pl.BlockSpec(memory_space=pltpu.HBM)
    arguments = (
        orbitals, occupation, assignment, pair_live,
        jnp.asarray(right), jnp.asarray(left), jnp.asarray(diagonal),
    )
    block = pltpu.VMEM((members, planes, points, points), jnp.float32)
    twice = pltpu.VMEM((pairs, 2, points // 2, points), jnp.float32)
    quad = pltpu.VMEM((pairs, 2, 2, points // 2, points), jnp.float32)
    column = pltpu.VMEM((planes, points, points), jnp.float32)
    dma = pltpu.SemaphoreType.DMA
    return pl.pallas_call(
        functools.partial(kernel, bands, slabs),
        out_shape=pltpu.VMEM(orbitals.shape, jnp.float32),
        in_specs=[hbm] * 7,
        out_specs=pl.BlockSpec(memory_space=pltpu.VMEM),
        scratch_shapes=[
            pltpu.SMEM(occupation.shape, occupation.dtype),
            pltpu.SMEM(assignment.shape, assignment.dtype),
            pltpu.SMEM(pair_live.shape, pair_live.dtype),
            pltpu.VMEM(right.shape, right.dtype),
            pltpu.VMEM(left.shape, left.dtype),
            pltpu.VMEM(diagonal.shape, diagonal.dtype),
            block, block, block, block,
            pltpu.VMEM((pairs, planes, points, points), jnp.float32),
            pltpu.VMEM((pairs, slabs // 2, points // 2, points), jnp.float32), twice,
            quad, twice, quad, twice, twice,
            column, column,
            pltpu.VMEM((11, points // 2, points), jnp.float32),
            pltpu.VMEM((slabs // 2, points // 2, points), jnp.float32),
            pltpu.VMEM((members, 2, points, points), jnp.float32),
            pltpu.VMEM((members, 8, points), jnp.float32),
            pltpu.VMEM((members, 8, points), jnp.float32),
            dma((members, chunks)), dma((members, chunks)), dma, dma, dma((members, chunks)), dma((members, chunks)),
            dma((pairs, slabs // 2)), dma((pairs, slabs // 2)),
            *[dma((pairs,)) for _ in range(4)],
            dma((7,)), pltpu.SemaphoreType.REGULAR, pltpu.SemaphoreType.REGULAR,
        ],
        compiler_params=pltpu.CompilerParams(
            collective_id=0, has_side_effects=True, vmem_limit_bytes=40000 * 1024
        ),
    )(*[pltpu.with_memory_space_constraint(a, pltpu.HBM) for a in arguments])


def solution(mesh):
    placed = (P("band", "slab", None, None), P(), P("band"), P("band", None))
    return jax.shard_map(
        functools.partial(local, mesh.shape["band"], mesh.shape["slab"]),
        mesh=mesh, in_specs=placed, out_specs=P("band", "slab", None, None), check_vma=False,
    )
```

```python
import functools

import jax
import jax.numpy as jnp
import numpy as np
from jax import lax
from jax.experimental import pallas as pl
from jax.experimental.pallas import tpu as pltpu
from jax.sharding import PartitionSpec as P

screening = 0.01
lateral = 0.01
MESH = pl.DeviceIdType.MESH


def tables(points):
    numbers = np.arange(points, dtype=np.float64) + 1.0
    sine = np.sqrt(2.0 / (points + 1.0)) * np.sin(
        np.pi * numbers[:, None] * numbers[None, :] / (points + 1.0)
    )
    eigen = 2.0 - 2.0 * np.cos(np.pi * numbers / (points + 1.0))
    sine = sine.astype(np.float32)
    high = sine.astype(jnp.bfloat16)
    low = (sine - high.astype(np.float32)).astype(jnp.bfloat16)
    half = np.concatenate([high, low], axis=1)
    right = np.concatenate([half, half], axis=0)
    diagonal = 2.0 + lateral * (eigen[:, None] + eigen[None, :]) + screening
    return right, np.ascontiguousarray(right.T), diagonal.astype(np.float32)


def split(value):
    high = value.astype(jnp.bfloat16)
    low = (value - high.astype(jnp.float32)).astype(jnp.bfloat16)
    return high, low


def plane_pair(first, second, right, left):
    points = first.shape[0]
    high, low = split(jnp.concatenate([first, second], axis=0))
    both = jnp.dot(
        jnp.concatenate([high, low], axis=1), right, preferred_element_type=jnp.float32
    )
    rows = both[:, :points] + both[:, points:]
    high, low = split(rows)
    stacked = jnp.concatenate(
        [
            jnp.concatenate([high[:points], high[points:]], axis=1),
            jnp.concatenate([low[:points], low[points:]], axis=1),
        ],
        axis=0,
    )
    both = jnp.dot(left, stacked, preferred_element_type=jnp.float32)
    result = both[:points] + both[points:]
    return result[:, :points], result[:, points:]


def chunks_of(planes):
    return max(1, min(4, planes // 4))


def kernel(
    bands, slabs,
    orbitals_hbm, occupation_hbm, assignment_hbm, live_hbm, right_hbm, left_hbm, diagonal_hbm,
    out,
    occupation, assignment, live, right_ref, left_ref, diagonal_ref,
    orbitals, visitors, visit_sum, returned, spectra, ends_in, ends_out,
    faces, face_out, edges, edge_out, merged,
    pivots, reach, coefs, ratios, bounds, weight_out, weight_in,
    send_orb, recv_orb, send_weight, recv_weight, send_back, recv_back,
    send_end, recv_end, send_face, recv_face, send_edge, recv_edge,
    load_sem, answer_sem, gather_sem,
):
    members, planes, points, _ = orbitals_hbm.shape
    pairs = members * members
    chunks = chunks_of(planes)
    depth = planes // chunks
    early = chunks // 2
    parts, share = chunks, depth
    load = pltpu.make_async_copy(orbitals_hbm, orbitals, load_sem.at[0])
    tables_in = [
        pltpu.make_async_copy(source, target, load_sem.at[n + 1])
        for n, (source, target) in enumerate((
            (occupation_hbm, occupation), (assignment_hbm, assignment), (live_hbm, live),
            (diagonal_hbm, diagonal_ref), (right_hbm, right_ref), (left_hbm, left_ref),
        ))
    ]
    band = lax.axis_index("band")
    slab = lax.axis_index("slab")
    above = lax.rem(band + 1, bands)
    below = lax.rem(band + bands - 1, bands)
    side = lax.rem(slab, 2)
    partner = slab + 1 - 2 * side
    duo, duos = slab // 2, slabs // 2
    half = points // 2
    mine = pl.ds(pl.multiple_of(side * half, half), half)
    other = pl.ds(pl.multiple_of((1 - side) * half, half), half)

    barrier = pltpu.get_barrier_semaphore()
    odd = lax.rem(band, 2) == 1
    even = jnp.logical_not(odd)

    def greet(semaphore, to_band, to_slab):
        pl.semaphore_signal(semaphore, inc=1, device_id=(to_band, to_slab), device_id_type=MESH)

    @pl.when(even)
    def _():
        greet(barrier, above, slab)
        greet(barrier, below, slab)

    for copy in tables_in:
        copy.start()
    load.start()
    tables_in[0].wait()
    tables_in[1].wait()
    weights = [occupation[assignment[k]] for k in range(members)]
    for k in range(members):
        weight_out[k] = jnp.full(weight_out.shape[1:], weights[k], jnp.float32)

    @pl.when(odd)
    def _():
        pl.semaphore_wait(barrier, 2)
        greet(answer_sem.at[0], below, slab)
        greet(answer_sem.at[1], above, slab)

    @pl.when(even)
    def _():
        pl.semaphore_wait(answer_sem.at[0], 1)
        greet(barrier, band, partner)

        @pl.loop(0, duos)
        def _(d):
            @pl.when(d != duo)
            def _():
                greet(barrier, band, 2 * d + side)

    def remote(source, target, sent, landed, device):
        return pltpu.make_async_remote_copy(
            src_ref=source, dst_ref=target, send_sem=sent, recv_sem=landed,
            device_id=device, device_id_type=MESH,
        )

    def orb_copy(k, c):
        span = pl.ds(c * depth, depth)
        return remote(
            orbitals_hbm.at[k, span], visitors.at[k, span],
            send_orb.at[k, c], recv_orb.at[k, c], (above, slab),
        )

    def back_copy(k, part):
        span = pl.ds(part * share, share)
        return remote(
            visit_sum.at[k, span], returned.at[k, span],
            send_back.at[k, part], recv_back.at[k, part], (below, slab),
        )

    def end_copy(p, d):
        way = (d < duo).astype(jnp.int32)
        return remote(
            ends_out.at[p, way], ends_in.at[p, duo], send_end.at[p, d], recv_end.at[p, duo],
            (band, 2 * d + side),
        )

    def end_arrival(p, d):
        return remote(
            ends_out.at[p, 0], ends_in.at[p, d], send_end.at[p, d], recv_end.at[p, d],
            (band, 2 * d + side),
        )

    def face_copy(p):
        return remote(face_out.at[p], faces.at[p, side], send_face.at[p], recv_face.at[p], (band, partner))

    def edge_copy(p):
        return remote(edge_out.at[p], edges.at[p, side], send_edge.at[p], recv_edge.at[p], (band, partner))

    weight_copy = remote(weight_out, weight_in, send_weight, recv_weight, (above, slab))
    weight_copy.start()
    for k in range(members):
        for c in range(chunks):
            orb_copy(k, c).start()
    for copy in tables_in[2:]:
        copy.wait()

    diagonal = diagonal_ref[...]
    pivot = 1.0 / diagonal
    pivots[0] = pivot
    for z in range(1, planes):
        pivot = 1.0 / (diagonal - pivot)
        pivots[z] = pivot
    response = pivot
    reach[planes - 1] = response
    for z in range(planes - 2, -1, -1):
        response = response * pivots[z]
        reach[z] = response
    near, far = reach[planes - 1, mine, :], reach[0, mine, :]
    inner = 1.0 / (1.0 - near * near)
    near_two = near + far * far * near * inner
    far_two = far * far * inner

    def chain(d, value):
        gap = 1.0 - value * near_two
        ratios[d] = far_two / gap
        coefs[0] = jnp.where(d == duo, value, coefs[0])
        coefs[1] = jnp.where(d == duos - 1 - duo, value, coefs[1])
        return near_two + far_two * far_two * value / gap

    coefs[0] = jnp.zeros_like(near)
    coefs[1] = jnp.zeros_like(near)
    lax.fori_loop(0, duos, chain, jnp.zeros_like(near))
    close_left, close_right = coefs[0], coefs[1]
    gap_left = 1.0 - close_left * near_two
    gap_right = 1.0 - close_right * near_two
    scale = 1.0 / (gap_left * gap_right - close_left * close_right * far_two * far_two)
    coefs[2] = far_two / gap_left
    coefs[3] = far_two / gap_right
    coefs[4] = gap_right * scale
    coefs[5] = close_left * far_two * scale
    coefs[6] = gap_left * scale
    coefs[7] = close_right * far_two * scale
    coefs[8] = inner
    coefs[9] = near * inner
    coefs[10] = far

    @pl.loop(0, members)
    def _(k):
        @pl.loop(0, planes)
        def _(z):
            zero = jnp.zeros((points, points), jnp.float32)
            out[k, z] = zero

    @pl.when(even)
    def _():
        pl.semaphore_wait(barrier, duos)
        greet(gather_sem, above, slab)
        pl.semaphore_wait(answer_sem.at[1], 1)

    weight_copy.wait()
    load.wait()

    def forward(k, c):
        orb_copy(k, c).wait_recv()

        for i in range(members):
            p = k * members + i
            carry = spectra[p, c * depth - 1] if c else jnp.zeros((points, points), jnp.float32)
            for z in range(c * depth, (c + 1) * depth, 2):
                one, two = plane_pair(
                    orbitals[i, z] * visitors[k, z],
                    orbitals[i, z + 1] * visitors[k, z + 1],
                    right_ref[...], left_ref[...],
                )
                one = (one + carry) * pivots[z]
                spectra[p, z] = one
                carry = (two + one) * pivots[z + 1]
                spectra[p, z + 1] = carry

    def backward(p):
        def back(h, value):
            z = planes - 2 - h
            value = spectra[p, z] + pivots[z] * value
            spectra[p, z] = value
            return value

        lax.fori_loop(0, planes - 1, back, spectra[p, planes - 1], unroll=min(3, planes - 1))
        for n, z in enumerate((0, planes - 1)):
            face_out[p, n] = spectra[p, z, other, :]
            faces[p, side, n] = spectra[p, z, mine, :]
        face_copy(p).start()

    def merge(p):
        face_copy(p).wait_recv()
        head, tail = faces[p, 0, 1], faces[p, 1, 0]
        lower_end = faces[p, 0, 0] + coefs[10] * (coefs[8] * tail + coefs[9] * head)
        upper_end = faces[p, 1, 1] + coefs[10] * (coefs[8] * head + coefs[9] * tail)
        merged[p, 0], merged[p, 1] = lower_end, upper_end
        ends_out[p, 0] = upper_end + coefs[2] * (coefs[0] * lower_end)
        ends_out[p, 1] = lower_end + coefs[3] * (coefs[1] * upper_end)

        @pl.loop(0, duos)
        def _(d):
            @pl.when(d != duo)
            def _():
                end_copy(p, d).start()

    def finish(p):
        @pl.loop(0, duos)
        def _(d):
            @pl.when(d != duo)
            def _():
                end_arrival(p, d).wait_recv()

        nothing = jnp.zeros((half, points), jnp.float32)
        below_end = lax.fori_loop(
            0, duo, lambda d, value: ends_in[p, d] + ratios[d] * value, nothing
        )
        above_end = lax.fori_loop(
            0, duos - 1 - duo,
            lambda d, value: ends_in[p, duos - 1 - d] + ratios[d] * value, nothing,
        )
        from_left = below_end + coefs[0] * merged[p, 0]
        from_right = above_end + coefs[1] * merged[p, 1]
        beyond_left = coefs[4] * from_left + coefs[5] * from_right
        beyond_right = coefs[6] * from_right + coefs[7] * from_left
        head = faces[p, 0, 1] + coefs[10] * beyond_left
        tail = faces[p, 1, 0] + coefs[10] * beyond_right
        inner_left = coefs[8] * head + coefs[9] * tail
        inner_right = coefs[8] * tail + coefs[9] * head
        lower = side == 0
        edges[p, side, 0] = jnp.where(lower, beyond_left, inner_left)
        edges[p, side, 1] = jnp.where(lower, inner_right, beyond_right)
        edge_out[p, 0] = jnp.where(lower, inner_left, beyond_left)
        edge_out[p, 1] = jnp.where(lower, beyond_right, inner_right)
        edge_copy(p).start()

    def inverse(k):
        own_factors, visit_factors = [], []
        for i in range(members):
            p = k * members + i
            edge_copy(p).wait_recv()
            for n in range(2):
                bounds[i, n] = jnp.concatenate([edges[p, 0, n], edges[p, 1, n]], axis=0)
            planned = live[i, below * members + k].astype(jnp.float32)
            own_factors.append(weight_in[k, 0:1, :] * (-planned))
            visit_factors.append(-(planned * occupation[assignment[i]]))

        @pl.loop(0, parts)
        def _(part):
            for h in range(share // 2):
                z = part * share + 2 * h
                sums = [None, None]
                for i in range(members):
                    p = k * members + i
                    fields = [
                        spectra[p, z + n] + reach[planes - 1 - n - z] * bounds[i, 0]
                        + reach[z + n] * bounds[i, 1]
                        for n in range(2)
                    ]
                    fields = plane_pair(*fields, right_ref[...], left_ref[...])
                    for n, value in enumerate(fields):
                        out[i, z + n] += own_factors[i] * (value * visitors[k, z + n])
                        term = visit_factors[i] * (value * orbitals[i, z + n])
                        sums[n] = term if sums[n] is None else sums[n] + term
                for n in range(2):
                    visit_sum[k, z + n] = sums[n]
            back_copy(k, part).start()

    def each(k, stage):
        @pl.loop(0, members)
        def _(i):
            stage(k * members + i)

    lag = lax.rem(band, 2)

    def within(k):
        return jnp.logical_and(k >= 0, k < members)

    @pl.loop(0, members + 4)
    def _(k):
        meet, close, leave = k - 1 - lag, k - 1 - 2 * lag, k - 2 - 2 * lag
        entering, meeting, closing, leaving = [within(n) for n in (k, meet, close, leave)]

        @pl.when(entering)
        def _():
            for c in range(early):
                forward(k, c)

        @pl.when(meeting)
        def _():
            each(meet, merge)

        @pl.when(leaving)
        def _():
            inverse(leave)

        @pl.when(entering)
        def _():
            for c in range(early, chunks):
                forward(k, c)

            @pl.when(jnp.logical_and(odd, k == 0))
            def _():
                pl.semaphore_wait(gather_sem, 1)

            each(k, backward)

        @pl.when(closing)
        def _():
            each(close, finish)


    @pl.loop(0, pairs)
    def _(p):
        face_copy(p).wait_send()
        edge_copy(p).wait_send()

        @pl.loop(0, duos)
        def _(d):
            @pl.when(d != duo)
            def _():
                end_arrival(p, d).wait_send()

    @pl.loop(0, members)
    def _(k):
        @pl.loop(0, parts)
        def _(part):
            orb_copy(k, part).wait_send()
            back_copy(k, part).wait()

            @pl.loop(0, share, unroll=True)
            def _(n):
                z = part * share + n
                out[k, z] += returned[k, z]


def local(bands, slabs, orbitals, occupation, assignment, pair_live):
    members, planes, points, _ = orbitals.shape
    pairs = members * members
    chunks = chunks_of(planes)
    right, left, diagonal = tables(points)
    hbm = pl.BlockSpec(memory_space=pltpu.HBM)
    arguments = (
        orbitals, occupation, assignment, pair_live,
        jnp.asarray(right), jnp.asarray(left), jnp.asarray(diagonal),
    )
    block = pltpu.VMEM((members, planes, points, points), jnp.float32)
    twice = pltpu.VMEM((pairs, 2, points // 2, points), jnp.float32)
    quad = pltpu.VMEM((pairs, 2, 2, points // 2, points), jnp.float32)
    column = pltpu.VMEM((planes, points, points), jnp.float32)
    dma = pltpu.SemaphoreType.DMA
    return pl.pallas_call(
        functools.partial(kernel, bands, slabs),
        out_shape=pltpu.VMEM(orbitals.shape, jnp.float32),
        in_specs=[hbm] * 7,
        out_specs=pl.BlockSpec(memory_space=pltpu.VMEM),
        scratch_shapes=[
            pltpu.SMEM(occupation.shape, occupation.dtype),
            pltpu.SMEM(assignment.shape, assignment.dtype),
            pltpu.SMEM(pair_live.shape, pair_live.dtype),
            pltpu.VMEM(right.shape, right.dtype),
            pltpu.VMEM(left.shape, left.dtype),
            pltpu.VMEM(diagonal.shape, diagonal.dtype),
            block, block, block, block,
            pltpu.VMEM((pairs, planes, points, points), jnp.float32),
            pltpu.VMEM((pairs, slabs // 2, points // 2, points), jnp.float32), twice,
            quad, twice, quad, twice, twice,
            column, column,
            pltpu.VMEM((11, points // 2, points), jnp.float32),
            pltpu.VMEM((slabs // 2, points // 2, points), jnp.float32),
            pltpu.VMEM((members, 2, points, points), jnp.float32),
            pltpu.VMEM((members, 8, points), jnp.float32),
            pltpu.VMEM((members, 8, points), jnp.float32),
            dma((members, chunks)), dma((members, chunks)), dma, dma, dma((members, chunks)), dma((members, chunks)),
            dma((pairs, slabs // 2)), dma((pairs, slabs // 2)),
            *[dma((pairs,)) for _ in range(4)],
            dma((7,)), pltpu.SemaphoreType.REGULAR((2,)), pltpu.SemaphoreType.REGULAR,
        ],
        compiler_params=pltpu.CompilerParams(
            collective_id=0, has_side_effects=True, vmem_limit_bytes=40000 * 1024
        ),
    )(*[pltpu.with_memory_space_constraint(a, pltpu.HBM) for a in arguments])


def solution(mesh):
    placed = (P("band", "slab", None, None), P(), P("band"), P("band", None))
    return jax.shard_map(
        functools.partial(local, mesh.shape["band"], mesh.shape["slab"]),
        mesh=mesh, in_specs=placed, out_specs=P("band", "slab", None, None), check_vma=False,
    )
```

```python
import functools

import jax
import jax.numpy as jnp
import numpy as np
from jax import lax
from jax.experimental import pallas as pl
from jax.experimental.pallas import tpu as pltpu
from jax.sharding import PartitionSpec as P

screening = 0.01
lateral = 0.01
MESH = pl.DeviceIdType.MESH


def tables(points):
    numbers = np.arange(points, dtype=np.float64) + 1.0
    sine = np.sqrt(2.0 / (points + 1.0)) * np.sin(
        np.pi * numbers[:, None] * numbers[None, :] / (points + 1.0)
    )
    eigen = 2.0 - 2.0 * np.cos(np.pi * numbers / (points + 1.0))
    sine = sine.astype(np.float32)
    high = sine.astype(jnp.bfloat16)
    low = (sine - high.astype(np.float32)).astype(jnp.bfloat16)
    half = np.concatenate([high, low], axis=1)
    right = np.concatenate([half, half], axis=0)
    diagonal = 2.0 + lateral * (eigen[:, None] + eigen[None, :]) + screening
    return right, np.ascontiguousarray(right.T), diagonal.astype(np.float32)


def split(value):
    high = value.astype(jnp.bfloat16)
    low = (value - high.astype(jnp.float32)).astype(jnp.bfloat16)
    return high, low


def plane_pair(first, second, right, left):
    points = first.shape[0]
    high, low = split(jnp.concatenate([first, second], axis=0))
    both = jnp.dot(
        jnp.concatenate([high, low], axis=1), right, preferred_element_type=jnp.float32
    )
    rows = both[:, :points] + both[:, points:]
    high, low = split(rows)
    stacked = jnp.concatenate(
        [
            jnp.concatenate([high[:points], high[points:]], axis=1),
            jnp.concatenate([low[:points], low[points:]], axis=1),
        ],
        axis=0,
    )
    both = jnp.dot(left, stacked, preferred_element_type=jnp.float32)
    result = both[:points] + both[points:]
    return result[:, :points], result[:, points:]


def chunks_of(planes):
    return max(1, min(4, planes // 4))


def kernel(
    bands, slabs,
    orbitals_hbm, occupation_hbm, assignment_hbm, live_hbm, right_hbm, left_hbm, diagonal_hbm,
    out,
    occupation, assignment, live, right_ref, left_ref, diagonal_ref,
    orbitals, visitors, visit_sum, returned, spectra, ends_in, ends_out,
    faces, face_out, edges, edge_out, merged,
    pivots, reach, coefs, ratios, bounds, weight_out, weight_in,
    send_orb, recv_orb, send_weight, recv_weight, send_back, recv_back,
    send_end, recv_end, send_face, recv_face, send_edge, recv_edge,
    load_sem, answer_sem, gather_sem,
):
    members, planes, points, _ = orbitals_hbm.shape
    pairs = members * members
    chunks = chunks_of(planes)
    depth = planes // chunks
    early = max(1, chunks // 4)
    parts, share = chunks, depth
    load = pltpu.make_async_copy(orbitals_hbm, orbitals, load_sem.at[0])
    tables_in = [
        pltpu.make_async_copy(source, target, load_sem.at[n + 1])
        for n, (source, target) in enumerate((
            (occupation_hbm, occupation), (assignment_hbm, assignment), (live_hbm, live),
            (diagonal_hbm, diagonal_ref), (right_hbm, right_ref), (left_hbm, left_ref),
        ))
    ]
    band = lax.axis_index("band")
    slab = lax.axis_index("slab")
    above = lax.rem(band + 1, bands)
    below = lax.rem(band + bands - 1, bands)
    side = lax.rem(slab, 2)
    partner = slab + 1 - 2 * side
    duo, duos = slab // 2, slabs // 2
    upper = duo // max(1, duos // 2)
    half = points // 2
    mine = pl.ds(pl.multiple_of(side * half, half), half)
    other = pl.ds(pl.multiple_of((1 - side) * half, half), half)

    barrier = pltpu.get_barrier_semaphore()
    odd = lax.rem(band, 2) == 1
    even = jnp.logical_not(odd)

    def greet(semaphore, to_band, to_slab):
        pl.semaphore_signal(semaphore, inc=1, device_id=(to_band, to_slab), device_id_type=MESH)

    @pl.when(even)
    def _():
        greet(barrier, above, slab)
        greet(barrier, below, slab)

    for copy in tables_in:
        copy.start()
    load.start()
    tables_in[0].wait()
    tables_in[1].wait()
    weights = [occupation[assignment[k]] for k in range(members)]
    for k in range(members):
        weight_out[k] = jnp.full(weight_out.shape[1:], weights[k], jnp.float32)

    @pl.when(odd)
    def _():
        pl.semaphore_wait(barrier, 2)
        greet(answer_sem.at[0], below, slab)
        greet(answer_sem.at[1], above, slab)

    @pl.when(even)
    def _():
        pl.semaphore_wait(answer_sem.at[0], 1)
        greet(barrier, band, partner)

        @pl.loop(0, duos)
        def _(d):
            @pl.when(d != duo)
            def _():
                greet(barrier, band, 2 * d + side)

    def remote(source, target, sent, landed, device):
        return pltpu.make_async_remote_copy(
            src_ref=source, dst_ref=target, send_sem=sent, recv_sem=landed,
            device_id=device, device_id_type=MESH,
        )

    def orb_copy(k, c):
        span = pl.ds(c * depth, depth)
        return remote(
            orbitals_hbm.at[k, span], visitors.at[k, span],
            send_orb.at[k, c], recv_orb.at[k, c], (above, slab),
        )

    def back_copy(k, part):
        span = pl.ds(part * share, share)
        return remote(
            visit_sum.at[k, span], returned.at[k, span],
            send_back.at[k, part], recv_back.at[k, part], (below, slab),
        )

    def end_copy(p, d):
        way = (d < duo).astype(jnp.int32)
        return remote(
            ends_out.at[p, way], ends_in.at[p, duo], send_end.at[p, d], recv_end.at[p, duo],
            (band, 2 * d + side),
        )

    def end_arrival(p, d):
        return remote(
            ends_out.at[p, 0], ends_in.at[p, d], send_end.at[p, d], recv_end.at[p, d],
            (band, 2 * d + side),
        )

    def face_copy(p):
        return remote(face_out.at[p], faces.at[p, side], send_face.at[p], recv_face.at[p], (band, partner))

    def edge_copy(p):
        return remote(edge_out.at[p], edges.at[p, side], send_edge.at[p], recv_edge.at[p], (band, partner))

    weight_copy = remote(weight_out, weight_in, send_weight, recv_weight, (above, slab))
    weight_copy.start()
    for k in range(members):
        for c in range(chunks):
            orb_copy(k, c).start()
    for copy in tables_in[2:]:
        copy.wait()

    diagonal = diagonal_ref[...]
    pivot = 1.0 / diagonal
    pivots[0] = pivot
    for z in range(1, planes):
        pivot = 1.0 / (diagonal - pivot)
        pivots[z] = pivot
    response = pivot
    reach[planes - 1] = response
    for z in range(planes - 2, -1, -1):
        response = response * pivots[z]
        reach[z] = response
    near, far = reach[planes - 1, mine, :], reach[0, mine, :]
    inner = 1.0 / (1.0 - near * near)
    near_two = near + far * far * near * inner
    far_two = far * far * inner

    def chain(d, value):
        gap = 1.0 - value * near_two
        ratios[d] = far_two / gap
        coefs[0] = jnp.where(d == duo, value, coefs[0])
        coefs[1] = jnp.where(d == duos - 1 - duo, value, coefs[1])
        return near_two + far_two * far_two * value / gap

    coefs[0] = jnp.zeros_like(near)
    coefs[1] = jnp.zeros_like(near)
    lax.fori_loop(0, duos, chain, jnp.zeros_like(near))
    close_left, close_right = coefs[0], coefs[1]
    gap_left = 1.0 - close_left * near_two
    gap_right = 1.0 - close_right * near_two
    scale = 1.0 / (gap_left * gap_right - close_left * close_right * far_two * far_two)
    coefs[2] = far_two / gap_left
    coefs[3] = far_two / gap_right
    coefs[4] = gap_right * scale
    coefs[5] = close_left * far_two * scale
    coefs[6] = gap_left * scale
    coefs[7] = close_right * far_two * scale
    coefs[8] = inner
    coefs[9] = near * inner
    coefs[10] = far

    @pl.loop(0, members)
    def _(k):
        @pl.loop(0, planes)
        def _(z):
            zero = jnp.zeros((points, points), jnp.float32)
            out[k, z] = zero

    @pl.when(even)
    def _():
        pl.semaphore_wait(barrier, duos)
        greet(gather_sem, above, slab)
        pl.semaphore_wait(answer_sem.at[1], 1)

    weight_copy.wait()
    load.wait()

    def forward(k, c):
        orb_copy(k, c).wait_recv()

        for i in range(members):
            p = k * members + i
            carry = spectra[p, c * depth - 1] if c else jnp.zeros((points, points), jnp.float32)
            for z in range(c * depth, (c + 1) * depth, 2):
                one, two = plane_pair(
                    orbitals[i, z] * visitors[k, z],
                    orbitals[i, z + 1] * visitors[k, z + 1],
                    right_ref[...], left_ref[...],
                )
                one = (one + carry) * pivots[z]
                spectra[p, z] = one
                carry = (two + one) * pivots[z + 1]
                spectra[p, z + 1] = carry

    def backward(p):
        def back(h, value):
            z = planes - 2 - h
            value = spectra[p, z] + pivots[z] * value
            spectra[p, z] = value
            return value

        lax.fori_loop(0, planes - 1, back, spectra[p, planes - 1], unroll=True)
        for n, z in enumerate((0, planes - 1)):
            face_out[p, n] = spectra[p, z, other, :]
            faces[p, side, n] = spectra[p, z, mine, :]
        face_copy(p).start()

    def merge(p):
        face_copy(p).wait_recv()
        head, tail = faces[p, 0, 1], faces[p, 1, 0]
        lower_end = faces[p, 0, 0] + coefs[10] * (coefs[8] * tail + coefs[9] * head)
        upper_end = faces[p, 1, 1] + coefs[10] * (coefs[8] * head + coefs[9] * tail)
        merged[p, 0], merged[p, 1] = lower_end, upper_end
        ends_out[p, 0] = upper_end + coefs[2] * (coefs[0] * lower_end)
        ends_out[p, 1] = lower_end + coefs[3] * (coefs[1] * upper_end)

        @pl.loop(0, duos)
        def _(t):
            d = upper * t + (1 - upper) * (duos - 1 - t)

            @pl.when(d != duo)
            def _():
                end_copy(p, d).start()

    def finish(p):
        @pl.loop(0, duos)
        def _(d):
            @pl.when(d != duo)
            def _():
                end_arrival(p, d).wait_recv()

        nothing = jnp.zeros((half, points), jnp.float32)
        below_end = lax.fori_loop(
            0, duo, lambda d, value: ends_in[p, d] + ratios[d] * value, nothing
        )
        above_end = lax.fori_loop(
            0, duos - 1 - duo,
            lambda d, value: ends_in[p, duos - 1 - d] + ratios[d] * value, nothing,
        )
        from_left = below_end + coefs[0] * merged[p, 0]
        from_right = above_end + coefs[1] * merged[p, 1]
        beyond_left = coefs[4] * from_left + coefs[5] * from_right
        beyond_right = coefs[6] * from_right + coefs[7] * from_left
        head = faces[p, 0, 1] + coefs[10] * beyond_left
        tail = faces[p, 1, 0] + coefs[10] * beyond_right
        inner_left = coefs[8] * head + coefs[9] * tail
        inner_right = coefs[8] * tail + coefs[9] * head
        lower = side == 0
        edges[p, side, 0] = jnp.where(lower, beyond_left, inner_left)
        edges[p, side, 1] = jnp.where(lower, inner_right, beyond_right)
        edge_out[p, 0] = jnp.where(lower, inner_left, beyond_left)
        edge_out[p, 1] = jnp.where(lower, beyond_right, inner_right)
        edge_copy(p).start()

    def inverse(k):
        own_factors, visit_factors = [], []
        for i in range(members):
            p = k * members + i
            edge_copy(p).wait_recv()
            for n in range(2):
                bounds[i, n] = jnp.concatenate([edges[p, 0, n], edges[p, 1, n]], axis=0)
            planned = live[i, below * members + k].astype(jnp.float32)
            own_factors.append(weight_in[k, 0:1, :] * (-planned))
            visit_factors.append(-(planned * occupation[assignment[i]]))

        @pl.loop(0, parts)
        def _(part):
            for h in range(share // 2):
                z = part * share + 2 * h
                sums = [None, None]
                for i in range(members):
                    p = k * members + i
                    fields = [
                        spectra[p, z + n] + reach[planes - 1 - n - z] * bounds[i, 0]
                        + reach[z + n] * bounds[i, 1]
                        for n in range(2)
                    ]
                    fields = plane_pair(*fields, right_ref[...], left_ref[...])
                    for n, value in enumerate(fields):
                        out[i, z + n] += own_factors[i] * (value * visitors[k, z + n])
                        term = visit_factors[i] * (value * orbitals[i, z + n])
                        sums[n] = term if sums[n] is None else sums[n] + term
                for n in range(2):
                    visit_sum[k, z + n] = sums[n]
            back_copy(k, part).start()

    def each(k, stage):
        @pl.loop(0, members)
        def _(i):
            stage(k * members + i)

    lag = lax.rem(band, 2)

    def within(k):
        return jnp.logical_and(k >= 0, k < members)

    @pl.loop(0, members + 4)
    def _(k):
        meet, close, leave = k - 1 - lag, k - 1 - 2 * lag, k - 2 - 2 * lag
        entering, meeting, closing, leaving = [within(n) for n in (k, meet, close, leave)]

        @pl.when(entering)
        def _():
            for c in range(early):
                forward(k, c)

        @pl.when(meeting)
        def _():
            each(meet, merge)

        @pl.when(leaving)
        def _():
            inverse(leave)

        @pl.when(entering)
        def _():
            for c in range(early, chunks):
                forward(k, c)

            @pl.when(jnp.logical_and(odd, k == 0))
            def _():
                pl.semaphore_wait(gather_sem, 1)

            each(k, backward)

        @pl.when(closing)
        def _():
            each(close, finish)


    @pl.loop(0, pairs)
    def _(p):
        face_copy(p).wait_send()
        edge_copy(p).wait_send()

        @pl.loop(0, duos)
        def _(d):
            @pl.when(d != duo)
            def _():
                end_arrival(p, d).wait_send()

    @pl.loop(0, members)
    def _(k):
        @pl.loop(0, parts)
        def _(part):
            orb_copy(k, part).wait_send()
            back_copy(k, part).wait()

            @pl.loop(0, share, unroll=True)
            def _(n):
                z = part * share + n
                out[k, z] += returned[k, z]


def local(bands, slabs, orbitals, occupation, assignment, pair_live):
    members, planes, points, _ = orbitals.shape
    pairs = members * members
    chunks = chunks_of(planes)
    right, left, diagonal = tables(points)
    hbm = pl.BlockSpec(memory_space=pltpu.HBM)
    arguments = (
        orbitals, occupation, assignment, pair_live,
        jnp.asarray(right), jnp.asarray(left), jnp.asarray(diagonal),
    )
    block = pltpu.VMEM((members, planes, points, points), jnp.float32)
    twice = pltpu.VMEM((pairs, 2, points // 2, points), jnp.float32)
    quad = pltpu.VMEM((pairs, 2, 2, points // 2, points), jnp.float32)
    column = pltpu.VMEM((planes, points, points), jnp.float32)
    dma = pltpu.SemaphoreType.DMA
    return pl.pallas_call(
        functools.partial(kernel, bands, slabs),
        out_shape=pltpu.VMEM(orbitals.shape, jnp.float32),
        in_specs=[hbm] * 7,
        out_specs=pl.BlockSpec(memory_space=pltpu.VMEM),
        scratch_shapes=[
            pltpu.SMEM(occupation.shape, occupation.dtype),
            pltpu.SMEM(assignment.shape, assignment.dtype),
            pltpu.SMEM(pair_live.shape, pair_live.dtype),
            pltpu.VMEM(right.shape, right.dtype),
            pltpu.VMEM(left.shape, left.dtype),
            pltpu.VMEM(diagonal.shape, diagonal.dtype),
            block, block, block, block,
            pltpu.VMEM((pairs, planes, points, points), jnp.float32),
            pltpu.VMEM((pairs, slabs // 2, points // 2, points), jnp.float32), twice,
            quad, twice, quad, twice, twice,
            column, column,
            pltpu.VMEM((11, points // 2, points), jnp.float32),
            pltpu.VMEM((slabs // 2, points // 2, points), jnp.float32),
            pltpu.VMEM((members, 2, points, points), jnp.float32),
            pltpu.VMEM((members, 8, points), jnp.float32),
            pltpu.VMEM((members, 8, points), jnp.float32),
            dma((members, chunks)), dma((members, chunks)), dma, dma, dma((members, chunks)), dma((members, chunks)),
            dma((pairs, slabs // 2)), dma((pairs, slabs // 2)),
            *[dma((pairs,)) for _ in range(4)],
            dma((7,)), pltpu.SemaphoreType.REGULAR((2,)), pltpu.SemaphoreType.REGULAR,
        ],
        compiler_params=pltpu.CompilerParams(
            collective_id=0, has_side_effects=True, vmem_limit_bytes=40000 * 1024
        ),
    )(*[pltpu.with_memory_space_constraint(a, pltpu.HBM) for a in arguments])


def solution(mesh):
    placed = (P("band", "slab", None, None), P(), P("band"), P("band", None))
    return jax.shard_map(
        functools.partial(local, mesh.shape["band"], mesh.shape["slab"]),
        mesh=mesh, in_specs=placed, out_specs=P("band", "slab", None, None), check_vma=False,
    )
```
